32 devices in a mesh: tm: 4 (over y, core), chan: 8 (over z, x).
Axes of the slice: x: 2, y: 2, z: 4, core: 2. Of those that a mesh axis runs over, the one named last changes fastest.
Arguments:
- traces: bfloat16 [8, 1024, 1024], P('tm', 'chan'), may hold values from -6 to 6
- lengths: int32 [8], replicated, may hold values from 512 to 1024
- source_blocks: int32 [3], replicated, may hold values from 0 to 31
Outputs:
- stacks: float32 [32, 3, 201, 1024], P('tm', None, None, 'chan')
The draws below stay inside these ranges and needn't reach their ends.
Inputs may be any that keep to these rules, and one draw needn't show every extreme that they name: Step s takes the source channels 32 * source_blocks[s] to 32 * source_blocks[s] + 31. `lengths`: samples at and after a segment's length are not used.
All inputs are finite; a program needn't handle non-finite values.
Results may differ from the reference program's by a relative error of at most 0.0085.
Values may be sent and summed in bfloat16 or wider, within the bound.
No kernel may reach another device: no remote copies, remote signals or barrier semaphores. Data moves between devices by JAX's collectives and lax.ppermute only.
A program may use at most 256 MiB of HBM per device.

```python
import jax
import jax.numpy as jnp
from jax import lax

SAMP = 1024
MAXLAG = 100
SRC = 32
STEPS = 3
LAGS = 201
SEGS = 8
NCH = 1024
N_TM = 4


def touch_ends(result, rng, least, top_value):
    dims = result.shape
    index_at = [jax.random.randint(jax.random.fold_in(rng, axis), (), 0, dims[axis]) for axis in range(len(dims))]
    result = result.at[tuple(index_at)].set(least)
    longest = dims.index(max(dims))
    index_at[longest] = (index_at[longest] + 1) % dims[longest]
    return result.at[tuple(index_at)].set(top_value)


def block_scale(key, shape, shards, least, high):
    def one(position, blocks):
        draws = jax.random.uniform(jax.random.fold_in(jax.random.fold_in(key, 6), position), (blocks,), jnp.float32, least / len(shards), high / len(shards))
        return jnp.repeat(jnp.exp(draws), shape[position] // blocks).reshape((-1,) + (1,) * (len(shape) - position - 1))

    gain = one(*shards[0])
    for cut in shards[1:]:
        gain = gain * one(*cut)
    return gain


def gaussian(own_key, extent, deviation, reach, shards=(), kind=jnp.bfloat16):
    array = deviation * jax.random.normal(own_key, extent, jnp.float32)
    if shards:
        array = array * block_scale(own_key, extent, shards, -0.22, 0.18)
    return jnp.clip(array, -reach, reach).astype(kind)


def setup_inputs(seed: int = 0) -> dict:
    seeds = jax.random.split(jax.random.key(seed), 4)
    traces = gaussian(seeds[0], (SEGS, NCH, SAMP), 1.0, 6.0, ((0, 4), (1, 8)))
    lengths = touch_ends(jax.random.randint(seeds[1], (SEGS,), SAMP // 2, SAMP + 1), jax.random.fold_in(seeds[1], 1), SAMP // 2, SAMP).astype(jnp.int32)
    source_blocks = jax.random.randint(seeds[2], (STEPS,), 0, NCH // SRC).astype(jnp.int32)
    return dict(traces=traces, lengths=lengths, source_blocks=source_blocks)


epsilon = 1e-06

def whiten(traces, lengths):
    sample_len = traces.shape[2]
    positions = lax.broadcasted_iota(jnp.int32, (1, 1, sample_len), 2)
    valid_mask = (positions < lengths[:, None, None]).astype(jnp.float32)
    masked = traces.astype(jnp.float32) * valid_mask
    seg_count = lengths.astype(jnp.float32)[:, None, None]
    mean_power = lax.optimization_barrier(jnp.sum(masked * masked, axis=2, keepdims=True)) / seg_count
    return (masked / jnp.sqrt(mean_power + epsilon)).astype(jnp.bfloat16)

def reference(traces, lengths, source_blocks):
    whitened = whiten(traces, lengths)
    widened = whitened.astype(jnp.float32)
    root_count = jnp.sqrt(lengths.astype(jnp.float32))
    results = []
    for step_index in range(STEPS):
        first_channel = (source_blocks[step_index] * SRC).astype(jnp.int32)
        sources = lax.dynamic_slice_in_dim(widened, first_channel, SRC, 1)
        padded = jnp.pad(sources, ((0, 0), (0, 0), (MAXLAG, MAXLAG)))

        def one_lag(lag_value):
            shifted = lax.dynamic_slice_in_dim(padded, (2 * MAXLAG - lag_value).astype(jnp.int32), SAMP, 2)
            product = jnp.einsum('gnu,gcu->gnc', shifted, widened, precision=lax.Precision.HIGHEST)
            product = product / root_count[:, None, None]
            grouped = lax.optimization_barrier(jnp.sum(product.reshape(N_TM, SEGS // N_TM, SRC, NCH), axis=1))
            rounded = lax.optimization_barrier(grouped.astype(jnp.bfloat16))
            return lax.optimization_barrier(jnp.sum(rounded.astype(jnp.float32), axis=0))
        per_lag = lax.map(one_lag, jnp.arange(LAGS, dtype=jnp.int32))
        results.append(jnp.transpose(per_lag, (1, 0, 2)))
    return jnp.stack(results, axis=1)
```

```python
import functools

import jax
import jax.numpy as jnp
from jax import lax
from jax.experimental import pallas as pl
from jax.experimental.pallas import tpu as pltpu
from jax.sharding import PartitionSpec as P

MAXLAG = 100
SRC = 32
FINE = 16
LANES = 128
epsilon = 1e-06


def plan(samp):
    lags = 2 * MAXLAG + 1
    blocks = -(-lags // FINE)
    front = -(-MAXLAG // FINE) * FINE
    base = front - MAXLAG
    tail = -(-(base + FINE - 1) // FINE) * FINE
    rows = samp + (blocks - 1) * FINE + tail
    return lags, blocks, front, base, tail, rows


def extract_kernel(per_owner, blocks_ref, traces_ref, out_ref, buf, sems):
    steps = blocks_ref.shape[0]
    seg_dev = traces_ref.shape[0]
    samp = traces_ref.shape[2]
    chunks = samp // LANES
    copies = []
    for s in range(steps):
        first = pl.multiple_of(lax.rem(blocks_ref[s], per_owner) * SRC, SRC)
        for g in range(seg_dev):
            n = s * seg_dev + g
            copy = pltpu.make_async_copy(
                traces_ref.at[g, pl.ds(first, SRC), :], buf.at[n], sems.at[n]
            )
            copy.start()
            copies.append(copy)
    share = out_ref.shape[1] // (steps * seg_dev)
    for n, copy in enumerate(copies):
        copy.wait()
        for q in range(SRC // share):
            for p in range(chunks):
                out_ref[q * chunks + p, n * share:(n + 1) * share, :] = buf[
                    n, q * share:(q + 1) * share, p * LANES:(p + 1) * LANES
                ]


def extract(traces, source_blocks, n_tm):
    seg_dev, chans, samp = traces.shape
    steps = source_blocks.shape[0]
    chunks = samp // LANES
    share = SRC // n_tm
    return pl.pallas_call(
        functools.partial(extract_kernel, chans // SRC),
        out_shape=jax.ShapeDtypeStruct((n_tm * chunks, steps * seg_dev * share, LANES), traces.dtype),
        in_specs=[pl.BlockSpec(memory_space=pltpu.SMEM), pl.BlockSpec(memory_space=pl.ANY)],
        out_specs=pl.BlockSpec(memory_space=pltpu.VMEM),
        scratch_shapes=[
            pltpu.VMEM((steps * seg_dev, SRC, samp), traces.dtype),
            pltpu.SemaphoreType.DMA((steps * seg_dev,)),
        ],
        name="extract",
    )(source_blocks, traces)


def pick_kernel(per_owner, n_tm, n_chan, blocks_ref, got_ref, out_ref):
    steps = blocks_ref.shape[0]
    share = SRC // n_tm
    seg_dev = got_ref.shape[1] // (steps * share)
    for s in range(steps):
        owner = lax.div(blocks_ref[s], per_owner)
        for q in range(n_tm):
            for g in range(seg_dev):
                n = s * seg_dev + g
                row = ((q * seg_dev + g) * steps + s) * share
                out_ref[row:row + share, :] = got_ref[
                    q * n_chan + owner, n * share:(n + 1) * share, :
                ]


def pick(got, source_blocks, per_owner, n_tm, n_chan):
    return pl.pallas_call(
        functools.partial(pick_kernel, per_owner, n_tm, n_chan),
        out_shape=jax.ShapeDtypeStruct((n_tm * got.shape[1], LANES), got.dtype),
        in_specs=[pl.BlockSpec(memory_space=pltpu.SMEM), pl.BlockSpec(memory_space=pltpu.VMEM)],
        out_specs=pl.BlockSpec(memory_space=pltpu.VMEM),
        name="pick",
    )(source_blocks, got)


def stack_kernel(n_parts, n_src, group, len_ref, pos_ref, *refs):
    parts = refs[:n_parts]
    pieces = refs[n_parts:n_parts + n_src]
    out_ref, src_buf, wpad, lhs, tailbuf = refs[n_parts + n_src:]
    seg_dev, chans, samp = parts[0].shape
    segs, nsrc, _ = src_buf.shape
    share = out_ref.shape[0]
    lags, blocks, front, base, tail, rows = plan(samp)
    bf = jnp.bfloat16
    per = LANES // tail
    tm_here = pos_ref[0]
    chan_here = pos_ref[1]
    if n_src == 1:
        src_buf[...] = pieces[0][...]
    else:
        for odd, piece in enumerate(pieces):
            for part in range(piece.shape[0]):
                start = pl.multiple_of((chan_here ^ (2 * part + odd)) * LANES, LANES)
                for g in range(segs):
                    src_buf[g, :, pl.ds(start, LANES)] = piece[part, g * nsrc:(g + 1) * nsrc, :]
    for slot in range(segs):
        m, local = slot // seg_dev, slot % seg_dev
        seg = (tm_here ^ m) * seg_dev + local
        count = len_ref[seg]
        countf = count.astype(jnp.float32)
        xt = parts[m][local].T.astype(jnp.float32)
        pos = lax.broadcasted_iota(jnp.int32, xt.shape, 0)
        xt = jnp.where(pos < count, xt, 0.0)
        power = jnp.sum(xt * xt, axis=0, keepdims=True) / countf
        scale = 1.0 / jnp.sqrt(power + epsilon)
        wpad[slot, 0:front, :] = jnp.zeros((front, chans), bf)
        wpad[slot, front:front + samp, :] = (xt * scale).astype(bf)
        wpad[slot, front + samp:rows, :] = jnp.zeros((rows - front - samp, chans), bf)
    for slot in range(segs):
        m, local = slot // seg_dev, slot % seg_dev
        seg = (tm_here ^ m) * seg_dev + local
        count = len_ref[seg]
        countf = count.astype(jnp.float32)
        x = src_buf[seg].astype(jnp.float32)
        pos = lax.broadcasted_iota(jnp.int32, x.shape, 1)
        x = jnp.where(pos < count, x, 0.0)
        power = jnp.sum(x * x, axis=1, keepdims=True) / countf
        x = x / (jnp.sqrt(power + epsilon) * jnp.sqrt(countf))
        x = jnp.concatenate([x, jnp.zeros((nsrc, LANES), jnp.float32)], axis=1)
        for j in range(nsrc):
            row = jnp.broadcast_to(x[j:j + 1, :], (FINE, samp + LANES))
            t = pltpu.roll(row, base, 1, stride=1, stride_axis=0)
            lhs[j * FINE:(j + 1) * FINE, slot * samp:(slot + 1) * samp] = t[:, :samp].astype(bf)
            last = t[:, samp:]
            if slot % per:
                tailbuf[j] = tailbuf[j] + pltpu.roll(last, (slot % per) * tail, 1)
            else:
                tailbuf[j] = last
            if slot % per == per - 1 or slot == segs - 1:
                at = segs * samp + slot // per * LANES
                lhs[j * FINE:(j + 1) * FINE, at:at + LANES] = tailbuf[j].astype(bf)
    for k0 in range(0, blocks, group):
        ks = range(k0, min(k0 + group, blocks))

        def window(slot, start, n):
            return jnp.concatenate(
                [wpad[slot, start + k * FINE:start + k * FINE + n, :] for k in ks], axis=1
            )

        acc = jnp.dot(lhs[:, 0:samp], window(0, 0, samp), preferred_element_type=jnp.float32)
        for slot in range(1, segs):
            acc = acc + jnp.dot(
                lhs[:, slot * samp:(slot + 1) * samp],
                window(slot, 0, samp),
                preferred_element_type=jnp.float32,
            )
        if k0 * FINE < front:
            ends = jnp.concatenate([window(slot, samp, tail) for slot in range(segs)], axis=0)
            acc = acc + jnp.dot(
                lhs[:, segs * samp:segs * (samp + tail)], ends, preferred_element_type=jnp.float32
            )
        for n, k in enumerate(ks):
            high = min(FINE, lags - k * FINE)
            for j in range(nsrc):
                out_ref[j % share, j // share, k * FINE:k * FINE + high, :] = acc[
                    j * FINE:j * FINE + high, n * chans:(n + 1) * chans
                ]


def stack(parts, pieces, lengths, where, share, steps, group=2):
    seg_dev, chans, samp = parts[0].shape
    segs = seg_dev * len(parts)
    nsrc = share * steps
    lags, blocks, front, base, tail, rows = plan(samp)
    ends = -(-segs * tail // LANES) * LANES
    smem = pl.BlockSpec(memory_space=pltpu.SMEM)
    vmem = pl.BlockSpec(memory_space=pltpu.VMEM)
    return pl.pallas_call(
        functools.partial(stack_kernel, len(parts), len(pieces), group),
        out_shape=jax.ShapeDtypeStruct((share, steps, lags, chans), jnp.float32),
        in_specs=[smem, smem] + [vmem] * (len(parts) + len(pieces)),
        out_specs=vmem,
        scratch_shapes=[
            pltpu.VMEM((segs, nsrc, samp), jnp.bfloat16),
            pltpu.VMEM((segs, rows, chans), jnp.bfloat16),
            pltpu.VMEM((nsrc * FINE, segs * samp + ends), jnp.bfloat16),
            pltpu.VMEM((nsrc, FINE, LANES), jnp.float32),
        ],
        name="stack",
    )(lengths, where, *parts, *pieces)


def swap(value, axis, size, distance):
    return lax.ppermute(value, axis, [(i, i ^ distance) for i in range(size)])


def gather_tm(traces, n_tm):
    parts = {0: traces}
    bit = n_tm // 2
    while bit:
        for m in list(parts):
            parts[m | bit] = swap(parts[m], "tm", n_tm, bit)
        bit //= 2
    return [parts[m] for m in range(n_tm)]


def shards(n_tm, n_chan, traces, lengths, source_blocks):
    seg_dev, chans, samp = traces.shape
    steps = source_blocks.shape[0]
    per_owner = chans // SRC
    share = SRC // n_tm
    nsrc = steps * share
    where = jnp.stack([lax.axis_index("tm"), lax.axis_index("chan")]).astype(jnp.int32)
    parts = gather_tm(traces, n_tm)
    if n_chan * LANES == samp and n_chan & (n_chan - 1) == 0:
        sent = extract(traces, source_blocks, n_tm)
        got = lax.all_to_all(sent, ("tm", "chan"), 0, 0)
        own = pick(got, source_blocks, per_owner, n_tm, n_chan)[None]
        held = own
        bit = 2
        while bit < n_chan:
            held = jnp.concatenate([held, swap(held, "chan", n_chan, bit)])
            bit *= 2
        pieces = [held, swap(held, "chan", n_chan, 1)]
    else:
        me = lax.axis_index("chan")
        contributions = []
        for s in range(steps):
            owner = source_blocks[s] // per_owner
            first = source_blocks[s] % per_owner * SRC
            block = lax.dynamic_slice_in_dim(traces, first, SRC, 1).astype(jnp.float32)
            contributions.append(jnp.where(owner == me, block, jnp.zeros_like(block)))
        summed = lax.psum(jnp.stack(contributions), "chan").astype(traces.dtype)
        split = jnp.moveaxis(summed.reshape(steps, seg_dev, n_tm, share, samp), 2, 0)
        moved = lax.all_to_all(split, "tm", 0, 0)
        pieces = [jnp.moveaxis(moved, 1, 2).reshape(n_tm * seg_dev, nsrc, samp)]
    return stack(parts, pieces, lengths, where, share, steps)


def solution(mesh):
    return jax.shard_map(
        functools.partial(shards, mesh.shape["tm"], mesh.shape["chan"]),
        mesh=mesh,
        in_specs=(P("tm", "chan", None), P(), P()),
        out_specs=P("tm", None, None, "chan"),
        check_vma=False,
    )
```

```python
import functools

import jax
import jax.numpy as jnp
from jax import lax
from jax.experimental import pallas as pl
from jax.experimental.pallas import tpu as pltpu
from jax.sharding import Mesh
from jax.sharding import PartitionSpec as P

MAXLAG = 100
SRC = 32
FINE = 16
LANES = 128
GROUP = 2
NEAR = 4
epsilon = 1e-06

SMEM = pl.BlockSpec(memory_space=pltpu.SMEM)
VMEM = pl.BlockSpec(memory_space=pltpu.VMEM)
HBM = pl.BlockSpec(memory_space=pltpu.HBM)
SMALL = pltpu.CompilerParams(vmem_limit_bytes=8 << 20)
WHOLE = pltpu.CompilerParams(vmem_limit_bytes=60 << 20)
LARGE = pltpu.CompilerParams(vmem_limit_bytes=28 << 20)


def plan(samp):
    lags = 2 * MAXLAG + 1
    blocks = -(-lags // FINE)
    front = -(-MAXLAG // FINE) * FINE
    base = front - MAXLAG
    tail = -(-(base + FINE - 1) // FINE) * FINE
    rows = samp + (blocks - 1) * FINE + tail
    return lags, blocks, front, base, tail, rows


def extract_kernel(per_owner, blocks_hbm, traces_ref, out_ref, owner_ref, blocks_ref, buf, sems):
    steps = blocks_ref.shape[0]
    seg_dev, _, samp = traces_ref.shape
    _, rows, width = out_ref.shape
    share = rows // steps
    load = pltpu.make_async_copy(blocks_hbm, blocks_ref, sems.at[steps * seg_dev])
    load.start()
    load.wait()
    copies = []
    for s in range(steps):
        first = pl.multiple_of(lax.rem(blocks_ref[s], per_owner) * SRC, SRC)
        for g in range(seg_dev):
            n = s * seg_dev + g
            copy = pltpu.make_async_copy(
                traces_ref.at[g, pl.ds(first, SRC), :], buf.at[n], sems.at[n]
            )
            copy.start()
            copies.append(copy)
        owner_ref[s] = jnp.full(owner_ref.shape[1:], lax.div(blocks_ref[s], per_owner), jnp.int32)
    for s in range(steps):
        for g in range(seg_dev):
            n = s * seg_dev + g
            copies[n].wait()
            for q in range(SRC // share):
                for h in range(samp // width):
                    out_ref[(q * (samp // width) + h) * seg_dev + g, s * share:(s + 1) * share, :] = buf[
                        n, q * share:(q + 1) * share, h * width:(h + 1) * width
                    ]


def extract(traces, source_blocks, n_tm):
    seg_dev, chans, samp = traces.shape
    steps = source_blocks.shape[0]
    share = SRC // n_tm
    return pl.pallas_call(
        functools.partial(extract_kernel, chans // SRC),
        out_shape=(
            jax.ShapeDtypeStruct((n_tm * 2 * seg_dev, steps * share, samp // 2), traces.dtype),
            jax.ShapeDtypeStruct((steps, share, LANES), jnp.int32),
        ),
        in_specs=[HBM, HBM],
        out_specs=(VMEM, VMEM),
        scratch_shapes=[
            pltpu.SMEM((steps,), jnp.int32),
            pltpu.VMEM((steps * seg_dev, SRC, samp), traces.dtype),
            pltpu.SemaphoreType.DMA((steps * seg_dev + 1,)),
        ],
        compiler_params=WHOLE,
        name="extract",
    )(source_blocks, traces)


def pick_kernel(owner_ref, got_ref, out_ref):
    steps, share, _ = owner_ref.shape
    n_tm, _, width = out_ref.shape
    near = got_ref.shape[0] // n_tm
    for s in range(steps):
        rows = slice(s * share, (s + 1) * share)
        owner = owner_ref[s] & (near - 1)
        for q in range(n_tm):
            for c in range(0, width, LANES):
                taken = got_ref[q * near, rows, c:c + LANES].astype(jnp.float32)
                for b in range(1, near):
                    other = got_ref[q * near + b, rows, c:c + LANES].astype(jnp.float32)
                    taken = jnp.where(owner == b, other, taken)
                out_ref[q, rows, c:c + LANES] = taken.astype(out_ref.dtype)


def pick(got, owners, n_tm):
    return pl.pallas_call(
        pick_kernel,
        out_shape=jax.ShapeDtypeStruct((n_tm,) + got.shape[1:], got.dtype),
        in_specs=[VMEM, VMEM],
        out_specs=VMEM,
        compiler_params=SMALL,
        name="pick",
    )(owners, got)


def choose_kernel(bit, owner_ref, held_ref, came_ref, out_ref):
    steps, share, _ = owner_ref.shape
    n_tm, _, width = out_ref.shape
    here = lax.axis_index("zh") * NEAR
    for s in range(steps):
        rows = slice(s * share, (s + 1) * share)
        other = ((owner_ref[s] ^ here) & (bit * NEAR)) != 0
        for q in range(n_tm):
            for c in range(0, width, LANES):
                held = held_ref[q, rows, c:c + LANES].astype(jnp.float32)
                came = came_ref[q, rows, c:c + LANES].astype(jnp.float32)
                out_ref[q, rows, c:c + LANES] = jnp.where(other, came, held).astype(out_ref.dtype)


def choose(held, came, owners, bit):
    return pl.pallas_call(
        functools.partial(choose_kernel, bit),
        out_shape=jax.ShapeDtypeStruct(held.shape, held.dtype),
        in_specs=[VMEM, VMEM, VMEM],
        out_specs=VMEM,
        compiler_params=SMALL,
        name="choose",
    )(owners, held, came)


def prepare_kernel(distance, len_ref, part_ref, out_ref):
    seg_dev, chans, samp = part_ref.shape
    _, _, front, _, _, rows = plan(samp)
    for g in range(seg_dev):
        count = len_ref[(lax.axis_index("tm") ^ distance) * seg_dev + g]
        xt = part_ref[g].T.astype(jnp.float32)
        pos = lax.broadcasted_iota(jnp.int32, xt.shape, 0)
        xt = jnp.where(pos < count, xt, 0.0)
        power = jnp.sum(xt * xt, axis=0, keepdims=True) / count.astype(jnp.float32)
        scale = 1.0 / jnp.sqrt(power + epsilon)
        out_ref[g, 0:front, :] = jnp.zeros((front, chans), out_ref.dtype)
        out_ref[g, front:front + samp, :] = (xt * scale).astype(out_ref.dtype)
        out_ref[g, front + samp:rows, :] = jnp.zeros((rows - front - samp, chans), out_ref.dtype)


def prepare(part, lengths, distance):
    seg_dev, chans, samp = part.shape
    rows = plan(samp)[-1]
    return pl.pallas_call(
        functools.partial(prepare_kernel, distance),
        out_shape=jax.ShapeDtypeStruct((seg_dev, rows, chans), jnp.bfloat16),
        in_specs=[SMEM, VMEM],
        out_specs=VMEM,
        compiler_params=SMALL,
        cost_estimate=pl.CostEstimate(flops=0, bytes_accessed=4 << 20, transcendentals=0),
        name="prepare",
    )(lengths, part)


def correlate_kernel(n_parts, flip, first, steps, len_ref, near_ref, far_ref, *refs):
    parts = refs[:n_parts]
    if first:
        out_ref, lhs, tailbuf = refs[n_parts:]
        carry_ref = None
    else:
        carry_ref, out_ref, buf, lhs, tailbuf, sems = refs[n_parts:]
    seg_dev, rows, chans = parts[0].shape
    _, nsrc, half = near_ref.shape
    samp = 2 * half
    share = nsrc // steps
    lags, blocks, front, base, tail, rows = plan(samp)
    bf = jnp.bfloat16
    tm_here = lax.axis_index("tm")
    local = lax.axis_index("x") ^ flip
    low_here = lax.axis_index("zl") == 0
    for m in range(n_parts):
        q = tm_here ^ m
        count = len_ref[q * seg_dev + local]
        countf = count.astype(jnp.float32)
        near = near_ref[q].astype(jnp.float32)
        far = far_ref[q].astype(jnp.float32)
        x = jnp.concatenate(
            [jnp.where(low_here, near, far), jnp.where(low_here, far, near)], axis=1
        )
        pos = lax.broadcasted_iota(jnp.int32, x.shape, 1)
        x = jnp.where(pos < count, x, 0.0)
        power = jnp.sum(x * x, axis=1, keepdims=True) / countf
        x = x / (jnp.sqrt(power + epsilon) * jnp.sqrt(countf))
        x = jnp.concatenate([x, jnp.zeros((nsrc, LANES), jnp.float32)], axis=1)
        for s in range(steps):
            rowsx = x[s * share:(s + 1) * share]
            for r in range(0, FINE, 2):
                t = jnp.concatenate(
                    [pltpu.roll(rowsx, base + r + d, 1) for d in range(2)], axis=0
                )
                at = (s * FINE + r) * share
                lhs[at:at + 2 * share, m * samp:(m + 1) * samp] = t[:, :samp].astype(bf)
                last = t[:, samp:]
                if m:
                    last = tailbuf[at:at + 2 * share, :] + pltpu.roll(last, m * tail, 1)
                if m == n_parts - 1:
                    lhs[at:at + 2 * share, n_parts * samp:] = last.astype(bf)
                else:
                    tailbuf[at:at + 2 * share, :] = last
    copies = []
    for n, k0 in enumerate(range(0, blocks, GROUP)):
        ks = range(k0, min(k0 + GROUP, blocks))

        def window(m, start, n):
            return jnp.concatenate(
                [parts[m][local, start + k * FINE:start + k * FINE + n, :] for k in ks], axis=1
            )

        acc = jnp.dot(lhs[:, 0:samp], window(0, 0, samp), preferred_element_type=jnp.float32)
        for m in range(1, n_parts):
            acc = acc + jnp.dot(
                lhs[:, m * samp:(m + 1) * samp],
                window(m, 0, samp),
                preferred_element_type=jnp.float32,
            )
        if k0 * FINE < front:
            ends = jnp.concatenate([window(m, samp, tail) for m in range(n_parts)], axis=0)
            acc = acc + jnp.dot(
                lhs[:, n_parts * samp:n_parts * (samp + tail)], ends, preferred_element_type=jnp.float32
            )
        width = len(ks) * chans
        if first:
            out_ref[n, :, 0:width] = acc
            continue
        acc = acc + carry_ref[n, :, 0:width]
        for p, k in enumerate(ks):
            high = min(FINE, lags - k * FINE)
            for s in range(steps):
                block = acc[s * FINE * share:(s * FINE + high) * share, p * chans:(p + 1) * chans]
                buf[s, k * FINE:k * FINE + high, :, :] = block.reshape(high, share, chans)
        lag0, lag1 = k0 * FINE, min((ks[-1] + 1) * FINE, lags)
        copy = pltpu.make_async_copy(
            buf.at[:, lag0:lag1], out_ref.at[:, lag0:lag1], sems.at[n]
        )
        copy.start()
        copies.append(copy)
    for copy in copies:
        copy.wait()


def correlate(parts, near, far, lengths, steps, flip, carry=None):
    _, rows, chans = parts[0].shape
    _, nsrc, half = near.shape
    samp = 2 * half
    n_parts = len(parts)
    lags, blocks, _, _, tail, rows = plan(samp)
    groups = -(-blocks // GROUP)
    ends = -(-n_parts * tail // LANES) * LANES
    first = carry is None
    work = [
        pltpu.VMEM((nsrc * FINE, n_parts * samp + ends), jnp.bfloat16),
        pltpu.VMEM((nsrc * FINE, LANES), jnp.float32),
    ]
    if first:
        shape = (groups, nsrc * FINE, GROUP * chans)
    else:
        shape = (steps, lags, nsrc // steps, chans)
        work = [pltpu.VMEM(shape, jnp.float32)] + work + [pltpu.SemaphoreType.DMA((groups,))]
    return pl.pallas_call(
        functools.partial(correlate_kernel, n_parts, flip, first, steps),
        out_shape=jax.ShapeDtypeStruct(shape, jnp.float32),
        in_specs=[SMEM] + [VMEM] * (2 + n_parts) + ([] if first else [VMEM]),
        out_specs=VMEM if first else HBM,
        scratch_shapes=work,
        compiler_params=LARGE,
        cost_estimate=pl.CostEstimate(
            flops=2 * nsrc * FINE * blocks * chans * samp * n_parts, bytes_accessed=8 << 20, transcendentals=0
        ),
        name="correlate",
    )(lengths, near, far, *parts, *([] if first else [carry]))


def swap(value, axis, size, distance):
    return lax.ppermute(value, axis, [(i, i ^ distance) for i in range(size)])


def shards(n_tm, n_far, traces, lengths, source_blocks):
    steps = source_blocks.shape[0]
    sent, owners = extract(traces, source_blocks, n_tm)
    got = lax.all_to_all(sent, ("tm", "zl", "x"), 0, 0)
    held = pick(got, owners, n_tm)
    bit = 1
    while bit < n_far:
        came = swap(held, "zh", n_far, bit)
        held = choose(held, came, owners, bit)
        bit *= 2
    near = held
    far = swap(near, "zl", 2, 1)
    near_x = swap(near, "x", 2, 1)
    far_x = swap(far, "x", 2, 1)
    blocks = {0: traces}
    bit = n_tm // 2
    while bit:
        for m in list(blocks):
            blocks[m | bit] = swap(blocks[m], "tm", n_tm, bit)
        bit //= 2
    parts = []
    for m in range(n_tm):
        parts.append(prepare(blocks[m], lengths, m))
    carry = correlate(parts, near, far, lengths, steps, 0)
    out = correlate(parts, near_x, far_x, lengths, steps, 1, carry)
    return jnp.transpose(out, (2, 0, 1, 3))


def solution(mesh):
    n_tm, n_chan = mesh.shape["tm"], mesh.shape["chan"]
    split = Mesh(
        mesh.devices.reshape(n_tm, n_chan // NEAR, 2, 2), ("tm", "zh", "zl", "x")
    )
    chan = ("zh", "zl", "x")
    return jax.shard_map(
        functools.partial(shards, n_tm, n_chan // NEAR),
        mesh=split,
        in_specs=(P("tm", chan, None), P(), P()),
        out_specs=P("tm", None, None, chan),
        check_vma=False,
    )
```

```python
import functools

import jax
import jax.numpy as jnp
from jax import lax
from jax.experimental import pallas as pl
from jax.experimental.pallas import tpu as pltpu
from jax.sharding import Mesh
from jax.sharding import PartitionSpec as P

MAXLAG = 100
SRC = 32
FINE = 16
LANES = 128
GROUP = 4
NEAR = 4
epsilon = 1e-06

SMEM = pl.BlockSpec(memory_space=pltpu.SMEM)
VMEM = pl.BlockSpec(memory_space=pltpu.VMEM)
HBM = pl.BlockSpec(memory_space=pltpu.HBM)
SMALL = pltpu.CompilerParams(vmem_limit_bytes=8 << 20)
WHOLE = pltpu.CompilerParams(vmem_limit_bytes=60 << 20)
LARGE = pltpu.CompilerParams(vmem_limit_bytes=20 << 20)


def plan(samp):
    half = samp // 2
    pairs = MAXLAG + 1
    blocks = -(-pairs // FINE)
    front = -(-(MAXLAG // 2) // FINE) * FINE
    base = front - MAXLAG // 2
    tail = -(-(base + FINE - 1) // FINE) * FINE
    rows = half + (blocks - 1) * FINE + tail
    full = pairs // FINE
    groups = [list(range(k, min(k + GROUP, full))) for k in range(0, full, GROUP)]
    groups += [[full]] if full < blocks else []
    return half, pairs, groups, front, base, tail, rows


def extract_kernel(per_owner, blocks_hbm, traces_ref, out_ref, owner_ref, first_ref, blocks_ref, buf, sems):
    steps = blocks_ref.shape[0]
    seg_dev, _, samp = traces_ref.shape
    _, rows, width = out_ref.shape
    share = rows // steps
    here = lax.axis_index("x")
    load = pltpu.make_async_copy(blocks_hbm, blocks_ref, sems.at[0])
    load.start()
    loads = []
    for n in range(seg_dev):
        copy = pltpu.make_async_copy(traces_ref.at[here ^ n], buf.at[n], sems.at[1 + n])
        copy.start()
        loads.append(copy)
    load.wait()
    for s in range(steps):
        owner_ref[s] = jnp.full(owner_ref.shape[1:], lax.div(blocks_ref[s], per_owner), jnp.int32)
    loads[0].wait()
    store = pltpu.make_async_copy(buf.at[0], first_ref, sems.at[1 + seg_dev])
    store.start()
    for copy in loads[1:]:
        copy.wait()
    for s in range(steps):
        first = pl.multiple_of(lax.rem(blocks_ref[s], per_owner) * SRC, SRC)
        for g in range(seg_dev):
            taken = buf[here ^ g, pl.ds(first, SRC), :]
            for q in range(SRC // share):
                for h in range(samp // width):
                    out_ref[(q * (samp // width) + h) * seg_dev + g, s * share:(s + 1) * share, :] = taken[
                        q * share:(q + 1) * share, h * width:(h + 1) * width
                    ]
    store.wait()


def extract(traces, source_blocks, n_tm):
    seg_dev, chans, samp = traces.shape
    steps = source_blocks.shape[0]
    share = SRC // n_tm
    return pl.pallas_call(
        functools.partial(extract_kernel, chans // SRC),
        out_shape=(
            jax.ShapeDtypeStruct((n_tm * 2 * seg_dev, steps * share, samp // 2), traces.dtype),
            jax.ShapeDtypeStruct((steps, share, LANES), jnp.int32),
            jax.ShapeDtypeStruct((chans, samp), traces.dtype),
        ),
        in_specs=[HBM, HBM],
        out_specs=(VMEM, VMEM, HBM),
        scratch_shapes=[
            pltpu.SMEM((steps,), jnp.int32),
            pltpu.VMEM((seg_dev, chans, samp), traces.dtype),
            pltpu.SemaphoreType.DMA((seg_dev + 2,)),
        ],
        compiler_params=WHOLE,
        name="extract",
    )(source_blocks, traces)


def pick_kernel(owner_ref, order_ref, got_ref, out_ref):
    steps, share, _ = owner_ref.shape
    n_tm, nsrc, width = out_ref.shape
    near = got_ref.shape[0] // n_tm
    rows_done = []
    for q in range(n_tm):
        for s in range(steps):
            rows = slice(s * share, (s + 1) * share)
            owner = owner_ref[s] & (near - 1)
            lanes = []
            for c in range(0, width, LANES):
                taken = got_ref[q * near, rows, c:c + LANES].astype(jnp.float32)
                for b in range(1, near):
                    other = got_ref[q * near + b, rows, c:c + LANES].astype(jnp.float32)
                    taken = jnp.where(owner == b, other, taken)
                lanes.append(taken)
            rows_done.append(jnp.concatenate(lanes, axis=1))
    taken = jnp.concatenate(rows_done, axis=0).astype(jnp.bfloat16)
    parted = jnp.dot(taken, order_ref[...], preferred_element_type=jnp.float32)
    for q in range(n_tm):
        out_ref[q] = parted[q * nsrc:(q + 1) * nsrc].astype(out_ref.dtype)


def pick(got, owners, order, n_tm):
    return pl.pallas_call(
        pick_kernel,
        out_shape=jax.ShapeDtypeStruct((n_tm,) + got.shape[1:], got.dtype),
        in_specs=[VMEM] * 3,
        out_specs=VMEM,
        compiler_params=SMALL,
        name="pick",
    )(owners, order, got)


def choose_kernel(bit, owner_ref, held_ref, came_ref, out_ref):
    steps, share, _ = owner_ref.shape
    n_tm, _, width = out_ref.shape
    here = lax.axis_index("zh") * NEAR
    for s in range(steps):
        rows = slice(s * share, (s + 1) * share)
        other = ((owner_ref[s] ^ here) & (bit * NEAR)) != 0
        for q in range(n_tm):
            for c in range(0, width, LANES):
                held = held_ref[q, rows, c:c + LANES].astype(jnp.float32)
                came = came_ref[q, rows, c:c + LANES].astype(jnp.float32)
                out_ref[q, rows, c:c + LANES] = jnp.where(other, came, held).astype(out_ref.dtype)


def choose(held, came, owners, bit):
    return pl.pallas_call(
        functools.partial(choose_kernel, bit),
        out_shape=jax.ShapeDtypeStruct(held.shape, held.dtype),
        in_specs=[VMEM, VMEM, VMEM],
        out_specs=VMEM,
        compiler_params=SMALL,
        name="choose",
    )(owners, held, came)


def whitened(block, count, work):
    xt = block.T.astype(jnp.float32)
    half = xt.shape[0] // 2
    pos = lax.broadcasted_iota(jnp.int32, xt.shape, 0)
    xt = jnp.where(pos < count, xt, 0.0)
    power = jnp.sum(xt * xt, axis=0, keepdims=True) / jnp.asarray(count).astype(jnp.float32)
    work[0:2 * half, :] = xt * (1.0 / jnp.sqrt(power + epsilon))
    return (
        work[pl.ds(0, half, stride=2), :].astype(jnp.bfloat16),
        work[pl.ds(1, half, stride=2), :].astype(jnp.bfloat16),
    )


def pad_into(ref, even, odd, work):
    half, chans = even.shape
    _, _, _, front, _, _, rows = plan(2 * half)
    even = even.astype(jnp.float32)
    wide = odd.astype(jnp.float32)
    work[0:half, :] = even
    work[half:half + 8, :] = jnp.zeros((8, chans), jnp.float32)
    after = work[1:half + 1, :]
    ref[0, front:front + half, :] = (even - wide).astype(ref.dtype)
    ref[1, front:front + half, :] = odd
    ref[2, front:front + half, :] = (after - wide).astype(ref.dtype)
    row = lax.broadcasted_iota(jnp.int32, (FINE, chans), 0)
    last = jnp.where(row == FINE - 1, jnp.broadcast_to(work[0:1, :], (FINE, chans)), 0.0)
    for n in range(3):
        ref[n, 0:front, :] = jnp.zeros((front, chans), ref.dtype)
        ref[n, front + half:rows, :] = jnp.zeros((rows - front - half, chans), ref.dtype)
    ref[2, front - FINE:front, :] = last.astype(ref.dtype)


def prepare_here_kernel(
    len_ref, traces_ref, owner_ref, first_ref, second_ref, bare_ref, passed_ref, order_ref, count_ref, work
):
    seg_dev = traces_ref.shape[0]
    for n in range(len_ref.shape[0]):
        count_ref[n:n + 1, :] = jnp.full((1, count_ref.shape[1]), len_ref[n], jnp.int32)
    passed_ref[...] = owner_ref[...]
    width = order_ref.shape[0]
    source = lax.broadcasted_iota(jnp.int32, (width, width), 0)
    place = lax.broadcasted_iota(jnp.int32, (width, width), 1)
    wanted = jnp.where(place < width // 2, 2 * place, 2 * place - width + 1)
    order_ref[...] = (source == wanted).astype(jnp.float32).astype(order_ref.dtype)
    here = lax.axis_index("x")
    row = lax.axis_index("tm") * seg_dev
    even, odd = whitened(traces_ref[here], len_ref[row + here], work)
    pad_into(first_ref, even, odd, work)
    even, odd = whitened(traces_ref[here ^ 1], len_ref[row + (here ^ 1)], work)
    bare_ref[0] = even
    bare_ref[1] = odd
    pad_into(second_ref, even, odd, work)


def prepare_here(traces, owners, lengths):
    _, chans, samp = traces.shape
    half = samp // 2
    full = jax.ShapeDtypeStruct((3, plan(samp)[-1], chans), jnp.bfloat16)
    bare = jax.ShapeDtypeStruct((2, half, chans), jnp.bfloat16)
    return pl.pallas_call(
        prepare_here_kernel,
        out_shape=(
            full,
            full,
            bare,
            jax.ShapeDtypeStruct(owners.shape, owners.dtype),
            jax.ShapeDtypeStruct((half, half), jnp.bfloat16),
            jax.ShapeDtypeStruct((lengths.shape[0], LANES), jnp.int32),
        ),
        in_specs=[SMEM, VMEM, VMEM],
        out_specs=(VMEM,) * 6,
        scratch_shapes=[pltpu.VMEM((samp + FINE, chans), jnp.float32)],
        compiler_params=SMALL,
        cost_estimate=pl.CostEstimate(flops=0, bytes_accessed=4 << 20, transcendentals=0),
        name="prepare_here",
    )(lengths, traces, owners)


def prepare_there_kernel(distances, seg_dev, count_ref, *refs):
    count_parts = len(distances)
    work = refs[-1]
    for distance, part_ref, out_ref in zip(distances, refs[:count_parts], refs[count_parts:-1]):
        seg = (lax.axis_index("tm") ^ distance) * seg_dev + lax.axis_index("x")
        even, odd = whitened(part_ref[...], count_ref[pl.ds(seg, 1), 0:part_ref.shape[0]], work)
        pad_into(out_ref, even, odd, work)


def prepare_there(named, seg_dev, counts):
    chans, samp = next(iter(named.values())).shape
    full = jax.ShapeDtypeStruct((3, plan(samp)[-1], chans), jnp.bfloat16)
    done = pl.pallas_call(
        functools.partial(prepare_there_kernel, tuple(named), seg_dev),
        out_shape=(full,) * len(named),
        in_specs=[VMEM] * (1 + len(named)),
        out_specs=(VMEM,) * len(named),
        scratch_shapes=[pltpu.VMEM((samp + FINE, chans), jnp.float32)],
        compiler_params=SMALL,
        cost_estimate=pl.CostEstimate(
            flops=0, bytes_accessed=len(named) << 21, transcendentals=0
        ),
        name="prepare_there",
    )(counts, *named.values())
    return dict(zip(named, done))


def correlate_kernel(n_parts, flip, first, steps, count_ref, near_ref, far_ref, *refs):
    parts = list(refs[:n_parts])
    (pads, work), refs = refs[-2:], refs[:-2]
    if first:
        out_ref, lhs, tailbuf = refs[n_parts:]
        carry_ref = None
    else:
        carry_ref, out_ref, buf, lhs, tailbuf, sems = refs[n_parts:]
    seg_dev = count_ref.shape[0] // n_parts
    chans = parts[0].shape[-1]
    _, nsrc, width = near_ref.shape
    share = nsrc // steps
    half, pairs, groups, front, base, tail, _ = plan(2 * width)
    quarter = width // 2
    bf = jnp.bfloat16
    tm_here = lax.axis_index("tm")
    local = lax.axis_index("x") ^ flip
    low_here = lax.axis_index("zl") == 0

    def build(m):
        if parts[m].shape[0] == 2:
            pad_into(pads.at[m], parts[m][0], parts[m][1], work)
            parts[m] = pads.at[m]
        q = tm_here ^ m
        count = count_ref[pl.ds(q * seg_dev + local, 1), 0:1]
        countf = count.astype(jnp.float32)
        near = near_ref[q].astype(jnp.float32)
        far = far_ref[q].astype(jnp.float32)
        low, high = jnp.where(low_here, near, far), jnp.where(low_here, far, near)
        sides = []
        for parity in range(2):
            x = jnp.concatenate(
                [low[:, parity * quarter:(parity + 1) * quarter], high[:, parity * quarter:(parity + 1) * quarter]],
                axis=1,
            )
            pos = 2 * lax.broadcasted_iota(jnp.int32, x.shape, 1) + parity
            sides.append(jnp.where(pos < count, x, 0.0))
        even, odd = sides
        power = jnp.sum(even * even + odd * odd, axis=1, keepdims=True) / countf
        scale = 1.0 / (jnp.sqrt(power + epsilon) * jnp.sqrt(countf))
        even, odd = even * scale, odd * scale
        for n, x in enumerate((even, even + odd, odd)):
            x = jnp.concatenate([x, jnp.zeros((nsrc, LANES), jnp.float32)], axis=1)
            for s in range(steps):
                rowsx = x[s * share:(s + 1) * share]
                for r in range(0, FINE, 2):
                    t = jnp.concatenate(
                        [pltpu.roll(rowsx, base + r + d, 1) for d in range(2)], axis=0
                    )
                    at = slice((s * FINE + r) * share, (s * FINE + r + 2) * share)
                    lhs[n, at, m * half:(m + 1) * half] = t[:, :half].astype(bf)
                    last = t[:, half:]
                    if m:
                        last = tailbuf[n, at, :] + pltpu.roll(last, m * tail, 1)
                    if m == n_parts - 1:
                        lhs[n, at, n_parts * half:] = last.astype(bf)
                    else:
                        tailbuf[n, at, :] = last

    copies = []
    for group, ks in enumerate(groups):
        used = min(FINE, pairs - ks[0] * FINE)

        def window(m, n, start, size):
            return jnp.concatenate(
                [parts[m][n, start + k * FINE:start + k * FINE + size, :] for k in ks], axis=1
            )

        def shifted(n, lo, hi):
            if used == FINE:
                return lhs[n, :, lo:hi]
            return jnp.concatenate(
                [lhs[n, s * FINE * share:(s * FINE + used) * share, lo:hi] for s in range(steps)], axis=0
            )

        sums = []
        for n in range(3):
            total = None
            for m in range(n_parts):
                if not group and not n:
                    build(m)
                term = jnp.dot(
                    shifted(n, m * half, (m + 1) * half),
                    window(m, n, 0, half),
                    preferred_element_type=jnp.float32,
                )
                total = term if total is None else total + term
            if ks[0] * FINE < front:
                ends = jnp.concatenate([window(m, n, half, tail) for m in range(n_parts)], axis=0)
                total = total + jnp.dot(
                    shifted(n, n_parts * half, n_parts * (half + tail)), ends, preferred_element_type=jnp.float32
                )
            sums.append(total)
        across = len(ks) * chans
        both = [sums[0] + sums[1], sums[1] + sums[2]]
        height = both[0].shape[0]
        for parity in range(2):
            if first:
                out_ref[group, parity, 0:height, 0:across] = both[parity]
                continue
            acc = both[parity] + carry_ref[group, parity, 0:height, 0:across]
            for p, k in enumerate(ks):
                for s in range(steps):
                    for r in range(used):
                        lag = 2 * (k * FINE + r) + parity
                        if lag <= 2 * MAXLAG:
                            at = (s * used + r) * share
                            buf[s, lag] = acc[at:at + share, p * chans:(p + 1) * chans]
        if not first:
            lag0, lag1 = 2 * ks[0] * FINE, min(2 * (ks[-1] + 1) * FINE, 2 * MAXLAG + 1)
            copy = pltpu.make_async_copy(
                buf.at[:, lag0:lag1], out_ref.at[:, lag0:lag1], sems.at[group]
            )
            copy.start()
            copies.append(copy)
    for copy in copies:
        copy.wait()


def correlate(parts, near, far, counts, steps, flip, carry=None):
    chans = parts[0].shape[-1]
    _, nsrc, width = near.shape
    samp = 2 * width
    n_parts = len(parts)
    half, pairs, groups, _, _, tail, rows = plan(samp)
    ends = -(-n_parts * tail // LANES) * LANES
    first = carry is None
    work = [
        pltpu.VMEM((3, nsrc * FINE, n_parts * half + ends), jnp.bfloat16),
        pltpu.VMEM((3, nsrc * FINE, LANES), jnp.float32),
    ]
    if first:
        shape = (len(groups), 2, nsrc * FINE, GROUP * chans)
    else:
        shape = (steps, 2 * MAXLAG + 1, nsrc // steps, chans)
        work = [pltpu.VMEM(shape, jnp.float32)] + work + [pltpu.SemaphoreType.DMA((len(groups),))]
    work.append(pltpu.VMEM((n_parts, 3, rows, chans), jnp.bfloat16))
    work.append(pltpu.VMEM((samp + FINE, chans), jnp.float32))
    return pl.pallas_call(
        functools.partial(correlate_kernel, n_parts, flip, first, steps),
        out_shape=jax.ShapeDtypeStruct(shape, jnp.float32),
        in_specs=[VMEM] * (3 + n_parts) + ([] if first else [VMEM]),
        out_specs=VMEM if first else HBM,
        scratch_shapes=work,
        compiler_params=LARGE,
        cost_estimate=pl.CostEstimate(
            flops=3 * nsrc * pairs * chans * samp * n_parts, bytes_accessed=8 << 20, transcendentals=0
        ),
        name="correlate",
    )(counts, near, far, *parts, *([] if first else [carry]))


def swap(value, axis, size, distance):
    return lax.ppermute(value, axis, [(i, i ^ distance) for i in range(size)])


def shards(n_tm, n_far, traces, lengths, source_blocks):
    seg_dev = traces.shape[0]
    steps = source_blocks.shape[0]
    sent, owners, own = extract(traces, source_blocks, n_tm)
    got = lax.all_to_all(sent, ("tm", "zl", "x"), 0, 0)
    first, second, bare, owners, order, counts = prepare_here(traces, owners, lengths)
    held = pick(got, owners, order, n_tm)
    bit = 1
    while bit < n_far:
        came = swap(held, "zh", n_far, bit)
        held = choose(held, came, owners, bit)
        bit *= 2
    near = held
    far = swap(near, "zl", 2, 1)
    near_x = swap(near, "x", 2, 1)
    far_x = lax.ppermute(near, ("zl", "x"), [(i, i ^ 3) for i in range(NEAR)])
    firsts, seconds = {0: first}, {0: second}
    raw, bares = {0: own}, {0: bare}
    top = n_tm // 2
    bit = top
    while bit:
        for m in sorted(set(raw) | set(firsts)):
            if m | bit < top:
                firsts[m | bit] = swap(firsts[m], "tm", n_tm, bit)
            else:
                raw[m | bit] = swap(raw[m], "tm", n_tm, bit)
            if m | bit < top:
                seconds[m | bit] = swap(seconds[m], "tm", n_tm, bit)
            else:
                bares[m | bit] = swap(bares[m], "tm", n_tm, bit)
        bit //= 2
    firsts.update(prepare_there({m: raw[m] for m in raw if m}, seg_dev, counts))
    for m in bares:
        if m:
            seconds[m] = bares[m]
    carry = correlate([firsts[m] for m in range(n_tm)], near, far, counts, steps, 0)
    out = correlate([seconds[m] for m in range(n_tm)], near_x, far_x, counts, steps, 1, carry)
    return jnp.transpose(out, (2, 0, 1, 3))


def solution(mesh):
    n_tm, n_chan = mesh.shape["tm"], mesh.shape["chan"]
    split = Mesh(
        mesh.devices.reshape(n_tm, n_chan // NEAR, 2, 2), ("tm", "zh", "zl", "x")
    )
    chan = ("zh", "zl", "x")
    return jax.shard_map(
        functools.partial(shards, n_tm, n_chan // NEAR),
        mesh=split,
        in_specs=(P("tm", chan, None), P(), P()),
        out_specs=P("tm", None, None, chan),
        check_vma=False,
    )
```

```python
import functools

import jax
import jax.numpy as jnp
from jax import lax
from jax.experimental import pallas as pl
from jax.experimental.pallas import tpu as pltpu
from jax.sharding import Mesh
from jax.sharding import PartitionSpec as P

MAXLAG = 100
SRC = 32
FINE = 16
LANES = 128
GROUP = 4
NEAR = 4
epsilon = 1e-06

SMEM = pl.BlockSpec(memory_space=pltpu.SMEM)
VMEM = pl.BlockSpec(memory_space=pltpu.VMEM)
HBM = pl.BlockSpec(memory_space=pltpu.HBM)
SMALL = pltpu.CompilerParams(vmem_limit_bytes=8 << 20)
WHOLE = pltpu.CompilerParams(vmem_limit_bytes=60 << 20)
LARGE = pltpu.CompilerParams(vmem_limit_bytes=20 << 20)


def plan(samp):
    half = samp // 2
    pairs = MAXLAG + 1
    blocks = -(-pairs // FINE)
    front = -(-(MAXLAG // 2) // FINE) * FINE
    base = front - MAXLAG // 2
    tail = -(-(base + FINE - 1) // FINE) * FINE
    rows = half + (blocks - 1) * FINE + tail
    full = pairs // FINE
    groups = [list(range(k, min(k + GROUP, full))) for k in range(0, full, GROUP)]
    groups += [[full]] if full < blocks else []
    return half, pairs, groups, front, base, tail, rows


def extract_kernel(per_owner, blocks_hbm, traces_ref, out_ref, owner_ref, first_ref, blocks_ref, buf, sems):
    steps = blocks_ref.shape[0]
    seg_dev, _, samp = traces_ref.shape
    _, rows, width = out_ref.shape
    share = rows // steps
    here = lax.axis_index("x")
    load = pltpu.make_async_copy(blocks_hbm, blocks_ref, sems.at[0])
    load.start()
    loads = []
    for n in range(seg_dev):
        copy = pltpu.make_async_copy(traces_ref.at[here ^ n], buf.at[n], sems.at[1 + n])
        copy.start()
        loads.append(copy)
    load.wait()
    for s in range(steps):
        owner_ref[s] = jnp.full(owner_ref.shape[1:], lax.div(blocks_ref[s], per_owner), jnp.int32)
    loads[0].wait()
    store = pltpu.make_async_copy(buf.at[0], first_ref, sems.at[1 + seg_dev])
    store.start()
    for copy in loads[1:]:
        copy.wait()
    for s in range(steps):
        first = pl.multiple_of(lax.rem(blocks_ref[s], per_owner) * SRC, SRC)
        for g in range(seg_dev):
            taken = buf[here ^ g, pl.ds(first, SRC), :]
            for q in range(SRC // share):
                for h in range(samp // width):
                    out_ref[(q * seg_dev + g) * (samp // width) + h, s * share:(s + 1) * share, :] = taken[
                        q * share:(q + 1) * share, h * width:(h + 1) * width
                    ]
    store.wait()


def extract(traces, source_blocks, n_tm):
    seg_dev, chans, samp = traces.shape
    steps = source_blocks.shape[0]
    share = SRC // n_tm
    return pl.pallas_call(
        functools.partial(extract_kernel, chans // SRC),
        out_shape=(
            jax.ShapeDtypeStruct((n_tm * 2 * seg_dev, steps * share, samp // 2), traces.dtype),
            jax.ShapeDtypeStruct((steps, share, LANES), jnp.int32),
            jax.ShapeDtypeStruct((chans, samp), traces.dtype),
        ),
        in_specs=[HBM, HBM],
        out_specs=(VMEM, VMEM, HBM),
        scratch_shapes=[
            pltpu.SMEM((steps,), jnp.int32),
            pltpu.VMEM((seg_dev, chans, samp), traces.dtype),
            pltpu.SemaphoreType.DMA((seg_dev + 2,)),
        ],
        compiler_params=WHOLE,
        name="extract",
    )(source_blocks, traces)


def pick_kernel(owner_ref, order_ref, got_ref, out_ref):
    steps, share, _ = owner_ref.shape
    n_tm, nsrc, width = out_ref.shape
    near = got_ref.shape[0] // n_tm
    rows_done = []
    for q in range(n_tm):
        for s in range(steps):
            rows = slice(s * share, (s + 1) * share)
            owner = owner_ref[s] & (near - 1)
            lanes = []
            for c in range(0, width, LANES):
                taken = got_ref[q * near, rows, c:c + LANES].astype(jnp.float32)
                for b in range(1, near):
                    other = got_ref[q * near + b, rows, c:c + LANES].astype(jnp.float32)
                    taken = jnp.where(owner == b, other, taken)
                lanes.append(taken)
            rows_done.append(jnp.concatenate(lanes, axis=1))
    taken = jnp.concatenate(rows_done, axis=0).astype(jnp.bfloat16)
    parted = jnp.dot(taken, order_ref[...], preferred_element_type=jnp.float32)
    for q in range(n_tm):
        out_ref[q] = parted[q * nsrc:(q + 1) * nsrc].astype(out_ref.dtype)


def pick(got, owners, order, n_tm):
    return pl.pallas_call(
        pick_kernel,
        out_shape=jax.ShapeDtypeStruct((n_tm,) + got.shape[1:], got.dtype),
        in_specs=[VMEM] * 3,
        out_specs=VMEM,
        compiler_params=SMALL,
        name="pick",
    )(owners, order, got)


def choose_kernel(bit, owner_ref, held_ref, came_ref, out_ref):
    steps, share, _ = owner_ref.shape
    n_tm, _, width = out_ref.shape
    here = lax.axis_index("zh") * NEAR
    for s in range(steps):
        rows = slice(s * share, (s + 1) * share)
        other = ((owner_ref[s] ^ here) & (bit * NEAR)) != 0
        for q in range(n_tm):
            for c in range(0, width, LANES):
                held = held_ref[q, rows, c:c + LANES].astype(jnp.float32)
                came = came_ref[q, rows, c:c + LANES].astype(jnp.float32)
                out_ref[q, rows, c:c + LANES] = jnp.where(other, came, held).astype(out_ref.dtype)


def choose(held, came, owners, bit):
    return pl.pallas_call(
        functools.partial(choose_kernel, bit),
        out_shape=jax.ShapeDtypeStruct(held.shape, held.dtype),
        in_specs=[VMEM, VMEM, VMEM],
        out_specs=VMEM,
        compiler_params=SMALL,
        name="choose",
    )(owners, held, came)


def whitened(block, count, work):
    xt = block.T.astype(jnp.float32)
    half = xt.shape[0] // 2
    pos = lax.broadcasted_iota(jnp.int32, xt.shape, 0)
    xt = jnp.where(pos < count, xt, 0.0)
    power = jnp.sum(xt * xt, axis=0, keepdims=True) / jnp.asarray(count).astype(jnp.float32)
    work[0:2 * half, :] = xt * (1.0 / jnp.sqrt(power + epsilon))
    return (
        work[pl.ds(0, half, stride=2), :].astype(jnp.bfloat16),
        work[pl.ds(1, half, stride=2), :].astype(jnp.bfloat16),
    )


def pad_into(ref, even, odd, work):
    half, chans = even.shape
    _, _, _, front, _, _, rows = plan(2 * half)
    even = even.astype(jnp.float32)
    wide = odd.astype(jnp.float32)
    work[0:half, :] = even
    work[half:half + 8, :] = jnp.zeros((8, chans), jnp.float32)
    after = work[1:half + 1, :]
    ref[0, front:front + half, :] = (even - wide).astype(ref.dtype)
    ref[1, front:front + half, :] = odd
    ref[2, front:front + half, :] = (after - wide).astype(ref.dtype)
    row = lax.broadcasted_iota(jnp.int32, (FINE, chans), 0)
    last = jnp.where(row == FINE - 1, jnp.broadcast_to(work[0:1, :], (FINE, chans)), 0.0)
    for n in range(3):
        ref[n, 0:front, :] = jnp.zeros((front, chans), ref.dtype)
        ref[n, front + half:rows, :] = jnp.zeros((rows - front - half, chans), ref.dtype)
    ref[2, front - FINE:front, :] = last.astype(ref.dtype)


def prepare_here_kernel(
    len_ref, traces_ref, owner_ref, first_ref, second_ref, bare_ref, passed_ref, order_ref, count_ref, work
):
    seg_dev = traces_ref.shape[0]
    for n in range(len_ref.shape[0]):
        count_ref[n:n + 1, :] = jnp.full((1, count_ref.shape[1]), len_ref[n], jnp.int32)
    passed_ref[...] = owner_ref[...]
    width = order_ref.shape[0]
    source = lax.broadcasted_iota(jnp.int32, (width, width), 0)
    place = lax.broadcasted_iota(jnp.int32, (width, width), 1)
    wanted = jnp.where(place < width // 2, 2 * place, 2 * place - width + 1)
    order_ref[...] = (source == wanted).astype(jnp.float32).astype(order_ref.dtype)
    here = lax.axis_index("x")
    row = lax.axis_index("tm") * seg_dev
    even, odd = whitened(traces_ref[here], len_ref[row + here], work)
    pad_into(first_ref, even, odd, work)
    even, odd = whitened(traces_ref[here ^ 1], len_ref[row + (here ^ 1)], work)
    bare_ref[0] = even
    bare_ref[1] = odd
    pad_into(second_ref, even, odd, work)


def prepare_here(traces, owners, lengths):
    _, chans, samp = traces.shape
    half = samp // 2
    full = jax.ShapeDtypeStruct((3, plan(samp)[-1], chans), jnp.bfloat16)
    bare = jax.ShapeDtypeStruct((2, half, chans), jnp.bfloat16)
    return pl.pallas_call(
        prepare_here_kernel,
        out_shape=(
            full,
            full,
            bare,
            jax.ShapeDtypeStruct(owners.shape, owners.dtype),
            jax.ShapeDtypeStruct((half, half), jnp.bfloat16),
            jax.ShapeDtypeStruct((lengths.shape[0], LANES), jnp.int32),
        ),
        in_specs=[SMEM, VMEM, VMEM],
        out_specs=(VMEM,) * 6,
        scratch_shapes=[pltpu.VMEM((samp + FINE, chans), jnp.float32)],
        compiler_params=SMALL,
        cost_estimate=pl.CostEstimate(flops=0, bytes_accessed=4 << 20, transcendentals=0),
        name="prepare_here",
    )(lengths, traces, owners)


def prepare_there_kernel(distances, seg_dev, count_ref, *refs):
    count_parts = len(distances)
    work = refs[-1]
    for distance, part_ref, out_ref in zip(distances, refs[:count_parts], refs[count_parts:-1]):
        seg = (lax.axis_index("tm") ^ distance) * seg_dev + lax.axis_index("x")
        even, odd = whitened(part_ref[...], count_ref[pl.ds(seg, 1), 0:part_ref.shape[0]], work)
        pad_into(out_ref, even, odd, work)


def prepare_there(named, seg_dev, counts):
    chans, samp = next(iter(named.values())).shape
    full = jax.ShapeDtypeStruct((3, plan(samp)[-1], chans), jnp.bfloat16)
    done = pl.pallas_call(
        functools.partial(prepare_there_kernel, tuple(named), seg_dev),
        out_shape=(full,) * len(named),
        in_specs=[VMEM] * (1 + len(named)),
        out_specs=(VMEM,) * len(named),
        scratch_shapes=[pltpu.VMEM((samp + FINE, chans), jnp.float32)],
        compiler_params=SMALL,
        cost_estimate=pl.CostEstimate(
            flops=0, bytes_accessed=len(named) << 21, transcendentals=0
        ),
        name="prepare_there",
    )(counts, *named.values())
    return dict(zip(named, done))


def correlate_kernel(n_parts, flip, first, steps, count_ref, near_ref, far_ref, *refs):
    parts = list(refs[:n_parts])
    (pads, work), refs = refs[-2:], refs[:-2]
    if first:
        out_ref, lhs, tailbuf = refs[n_parts:]
        carry_ref = None
    else:
        carry_ref, out_ref, buf, lhs, tailbuf, sems = refs[n_parts:]
    seg_dev = count_ref.shape[0] // n_parts
    chans = parts[0].shape[-1]
    _, nsrc, width = near_ref.shape
    share = nsrc // steps
    half, pairs, groups, front, base, tail, _ = plan(2 * width)
    quarter = width // 2
    bf = jnp.bfloat16
    tm_here = lax.axis_index("tm")
    local = lax.axis_index("x") ^ flip
    low_here = lax.axis_index("zl") == 0

    def build(m):
        if parts[m].shape[0] == 2:
            pad_into(pads.at[m], parts[m][0], parts[m][1], work)
            parts[m] = pads.at[m]
        q = tm_here ^ m
        count = count_ref[pl.ds(q * seg_dev + local, 1), 0:1]
        countf = count.astype(jnp.float32)
        near = near_ref[q].astype(jnp.float32)
        far = far_ref[q].astype(jnp.float32)
        low, high = jnp.where(low_here, near, far), jnp.where(low_here, far, near)
        sides = []
        for parity in range(2):
            x = jnp.concatenate(
                [low[:, parity * quarter:(parity + 1) * quarter], high[:, parity * quarter:(parity + 1) * quarter]],
                axis=1,
            )
            pos = 2 * lax.broadcasted_iota(jnp.int32, x.shape, 1) + parity
            sides.append(jnp.where(pos < count, x, 0.0))
        even, odd = sides
        power = jnp.sum(even * even + odd * odd, axis=1, keepdims=True) / countf
        scale = 1.0 / (jnp.sqrt(power + epsilon) * jnp.sqrt(countf))
        even, odd = even * scale, odd * scale
        for n, x in enumerate((even, even + odd, odd)):
            x = jnp.concatenate([x, jnp.zeros((nsrc, LANES), jnp.float32)], axis=1)
            for s in range(steps):
                rowsx = x[s * share:(s + 1) * share]
                for r in range(0, FINE, 2):
                    t = jnp.concatenate(
                        [pltpu.roll(rowsx, base + r + d, 1) for d in range(2)], axis=0
                    )
                    at = slice((s * FINE + r) * share, (s * FINE + r + 2) * share)
                    lhs[n, at, m * half:(m + 1) * half] = t[:, :half].astype(bf)
                    last = t[:, half:]
                    if m:
                        last = tailbuf[n, at, :] + pltpu.roll(last, m * tail, 1)
                    if m == n_parts - 1:
                        lhs[n, at, n_parts * half:] = last.astype(bf)
                    else:
                        tailbuf[n, at, :] = last

    copies = []
    for group, ks in enumerate(groups):
        used = min(FINE, pairs - ks[0] * FINE)

        def window(m, n, start, size):
            return jnp.concatenate(
                [parts[m][n, start + k * FINE:start + k * FINE + size, :] for k in ks], axis=1
            )

        def shifted(n, lo, hi):
            if used == FINE:
                return lhs[n, :, lo:hi]
            return jnp.concatenate(
                [lhs[n, s * FINE * share:(s * FINE + used) * share, lo:hi] for s in range(steps)], axis=0
            )

        sums = []
        for n in range(3):
            total = None
            for m in range(n_parts):
                if not group and not n:
                    build(m)
                term = jnp.dot(
                    shifted(n, m * half, (m + 1) * half),
                    window(m, n, 0, half),
                    preferred_element_type=jnp.float32,
                )
                total = term if total is None else total + term
            if ks[0] * FINE < front:
                ends = jnp.concatenate([window(m, n, half, tail) for m in range(n_parts)], axis=0)
                total = total + jnp.dot(
                    shifted(n, n_parts * half, n_parts * (half + tail)), ends, preferred_element_type=jnp.float32
                )
            sums.append(total)
        across = len(ks) * chans
        both = [sums[0] + sums[1], sums[1] + sums[2]]
        height = both[0].shape[0]
        for parity in range(2):
            if first:
                out_ref[group, parity, 0:height, 0:across] = both[parity]
                continue
            acc = both[parity] + carry_ref[group, parity, 0:height, 0:across]
            for p, k in enumerate(ks):
                for s in range(steps):
                    for r in range(used):
                        lag = 2 * (k * FINE + r) + parity
                        if lag <= 2 * MAXLAG:
                            at = (s * used + r) * share
                            buf[s, lag] = acc[at:at + share, p * chans:(p + 1) * chans]
        if not first:
            lag0, lag1 = 2 * ks[0] * FINE, min(2 * (ks[-1] + 1) * FINE, 2 * MAXLAG + 1)
            copy = pltpu.make_async_copy(
                buf.at[:, lag0:lag1], out_ref.at[:, lag0:lag1], sems.at[group]
            )
            copy.start()
            copies.append(copy)
    for copy in copies:
        copy.wait()


def correlate(parts, near, far, counts, steps, flip, carry=None):
    chans = parts[0].shape[-1]
    _, nsrc, width = near.shape
    samp = 2 * width
    n_parts = len(parts)
    half, pairs, groups, _, _, tail, rows = plan(samp)
    ends = -(-n_parts * tail // LANES) * LANES
    first = carry is None
    work = [
        pltpu.VMEM((3, nsrc * FINE, n_parts * half + ends), jnp.bfloat16),
        pltpu.VMEM((3, nsrc * FINE, LANES), jnp.float32),
    ]
    if first:
        shape = (len(groups), 2, nsrc * FINE, GROUP * chans)
    else:
        shape = (steps, 2 * MAXLAG + 1, nsrc // steps, chans)
        work = [pltpu.VMEM(shape, jnp.float32)] + work + [pltpu.SemaphoreType.DMA((len(groups),))]
    work.append(pltpu.VMEM((n_parts, 3, rows, chans), jnp.bfloat16))
    work.append(pltpu.VMEM((samp + FINE, chans), jnp.float32))
    return pl.pallas_call(
        functools.partial(correlate_kernel, n_parts, flip, first, steps),
        out_shape=jax.ShapeDtypeStruct(shape, jnp.float32),
        in_specs=[VMEM] * (3 + n_parts) + ([] if first else [VMEM]),
        out_specs=VMEM if first else HBM,
        scratch_shapes=work,
        compiler_params=LARGE,
        cost_estimate=pl.CostEstimate(
            flops=3 * nsrc * pairs * chans * samp * n_parts, bytes_accessed=8 << 20, transcendentals=0
        ),
        name="correlate",
    )(counts, near, far, *parts, *([] if first else [carry]))


def swap(value, axis, size, distance):
    return lax.ppermute(value, axis, [(i, i ^ distance) for i in range(size)])


def shards(n_tm, n_far, traces, lengths, source_blocks):
    seg_dev = traces.shape[0]
    steps = source_blocks.shape[0]
    sent, owners, own = extract(traces, source_blocks, n_tm)
    got = lax.all_to_all(sent, ("tm", "x", "zl"), 0, 0)
    first, second, bare, owners, order, counts = prepare_here(traces, owners, lengths)
    held = pick(got, owners, order, n_tm)
    bit = 1
    while bit < n_far:
        came = swap(held, "zh", n_far, bit)
        held = choose(held, came, owners, bit)
        bit *= 2
    near = held
    far = swap(near, "zl", 2, 1)
    near_x = swap(near, "x", 2, 1)
    far_x = swap(far, "x", 2, 1)
    firsts, seconds = {0: first}, {0: second}
    raw, bares = {0: own}, {0: bare}
    top = n_tm // 2
    bit = top
    while bit:
        for m in sorted(set(raw) | set(firsts)):
            if m | bit < top:
                firsts[m | bit] = swap(firsts[m], "tm", n_tm, bit)
            else:
                raw[m | bit] = swap(raw[m], "tm", n_tm, bit)
            if m | bit < top:
                seconds[m | bit] = swap(seconds[m], "tm", n_tm, bit)
            else:
                bares[m | bit] = swap(bares[m], "tm", n_tm, bit)
        bit //= 2
    firsts.update(prepare_there({m: raw[m] for m in raw if m}, seg_dev, counts))
    for m in bares:
        if m:
            seconds[m] = bares[m]
    carry = correlate([firsts[m] for m in range(n_tm)], near, far, counts, steps, 0)
    out = correlate([seconds[m] for m in range(n_tm)], near_x, far_x, counts, steps, 1, carry)
    return jnp.transpose(out, (2, 0, 1, 3))


def solution(mesh):
    n_tm, n_chan = mesh.shape["tm"], mesh.shape["chan"]
    split = Mesh(
        mesh.devices.reshape(n_tm, n_chan // NEAR, 2, 2), ("tm", "zh", "x", "zl")
    )
    chan = ("zh", "x", "zl")
    return jax.shard_map(
        functools.partial(shards, n_tm, n_chan // NEAR),
        mesh=split,
        in_specs=(P("tm", chan, None), P(), P()),
        out_specs=P("tm", None, None, chan),
        check_vma=False,
    )
```
